256 devices in a mesh: wide: 32 (over x, y, core), narrow: 8 (over z).
Axes of the slice: x: 4, y: 4, z: 8, core: 2. Of those that a mesh axis runs over, the one named last changes fastest.
Arguments:
- corpus: float32 [524288, 1024], P(('wide', 'narrow')), may hold values from -30 to 30
- sketch: float32 [1024, 256], replicated, may hold values from -0.125 to 0.125
Outputs:
- basis: float32 [524288, 256], P(('wide', 'narrow'))
- projection: float32 [256, 1024], replicated
The draws below stay inside these ranges and needn't reach their ends.
All inputs are finite; a program needn't handle non-finite values.
Results may differ from the reference program's by a relative error of at most 0.0003.
Values sent between devices are 32-bit elements; how exact they have to be, the bound alone decides.
No kernel may reach another device: no remote copies, remote signals or barrier semaphores. Data moves between devices by JAX's collectives and lax.ppermute only.
A program may use at most 64 MiB of HBM per device.

```python
import jax
import jax.numpy as jnp
from jax import lax

D = 1024
K = 256
ROWS = 524288


def draw_corpus(key, part):
    keys = jax.random.split(jax.random.fold_in(key, 17), 4)
    position = jnp.arange(ROWS, dtype=jnp.float32) / ROWS
    order = jax.random.permutation(keys[3], D).astype(jnp.float32)
    ladder = jnp.minimum(order, K - 1.0) / (K - 1.0)
    noise = jnp.clip(jax.random.normal(keys[0], (ROWS, D), jnp.float32), -6.0, 6.0)
    jitter = jax.random.uniform(keys[2], (ROWS, 1), jnp.float32, 0.5, 1.5)
    column_scale = jnp.power(10.0, -3.0 * ladder)
    scale = (1.0 + 2.0 * position)[:, None] * jitter
    return scale * noise * column_scale[None, :]


def draw_sketch(key, part):
    inner = jax.random.fold_in(key, 29)
    values = jnp.clip(jax.random.normal(inner, (D, K), jnp.float32), -4.0, 4.0)
    return values / jnp.sqrt(jnp.float32(D))


def setup_inputs(seed: int = 0) -> dict:
    seeds = jax.random.split(jax.random.key(seed), 3)
    corpus = draw_corpus(jax.random.fold_in(seeds[2], 71), 0)
    sketch = draw_sketch(jax.random.fold_in(seeds[2], 71), 0)
    return dict(corpus=corpus, sketch=sketch)


def upper_factor(gram):
    return jnp.linalg.cholesky(gram).T

def reference(corpus, sketch):
    hi = lax.Precision.HIGHEST
    sample = jnp.dot(corpus.astype(jnp.float32), sketch.astype(jnp.float32), precision=hi, preferred_element_type=jnp.float32)
    first_r = upper_factor(jnp.dot(sample.T, sample, precision=hi))
    first_q = jax.scipy.linalg.solve_triangular(first_r.T, sample.T, lower=True).T
    second_r = upper_factor(jnp.dot(first_q.T, first_q, precision=hi))
    ortho = jax.scipy.linalg.solve_triangular(second_r.T, first_q.T, lower=True).T
    root = jnp.sqrt(jnp.float32(ROWS))
    basis = ortho * root
    projection = jnp.dot(ortho.T.astype(jnp.float32), corpus.astype(jnp.float32), precision=hi, preferred_element_type=jnp.float32) / root
    return (basis, projection)
```

```python
import math

import jax
import jax.numpy as jnp
from jax import lax
from jax.experimental import pallas as pl
from jax.experimental.pallas import tpu as pltpu
from jax.sharding import Mesh
from jax.sharding import PartitionSpec as P

WIDE_NARROW = ("wide_0", "wide_1", "wide_2", "narrow")
PLANE = ("wide_0", "wide_1")
CORE = "wide_2"
LINE = "narrow"
HI = lax.Precision.HIGHEST
F32 = jnp.float32
BF16 = jnp.bfloat16
ROWS_PER_STEP = 512
BLOCK = 64


def dot(a, b, dims=((1,), (0,)), precision=HI):
    return lax.dot_general(a, b, (dims, ((), ())), precision=precision, preferred_element_type=F32)


def dot16(a, b, dims=((1,), (0,))):
    return lax.dot_general(a, b, (dims, ((), ())), preferred_element_type=F32)


def split3(x):
    a = x.astype(BF16)
    r = x - a.astype(F32)
    b = r.astype(BF16)
    return a, b, (r - b.astype(F32)).astype(BF16)


def two_sum(a, b):
    s = a + b
    t = s - a
    return s, (a - (s - t)) + (b - t)


def grid_slices(x, top):
    out = []
    for i in range(4):
        edge = top * (2.0 ** (17 - 8 * i))
        a = (x + edge) - edge
        out.append(a.astype(BF16))
        x = x - a
    return out


def half_gram(s, top, rows):
    tn = ((0,), (0,))
    h = l = low = None
    for at in range(0, s.shape[0], rows):
        a = grid_slices(s[at : at + rows, :], top)
        terms = [0.5 * dot16(a[0], a[0], tn), dot16(a[0], a[1], tn)]
        rest = (dot16(a[0], a[2], tn) + 0.5 * dot16(a[1], a[1], tn)) + (
            (dot16(a[0], a[3], tn) + dot16(a[1], a[2], tn)) + (dot16(a[1], a[3], tn) + 0.5 * dot16(a[2], a[2], tn))
        )
        low = rest if low is None else low + rest
        for t in terms:
            if h is None:
                h = t
            else:
                h, e = two_sum(h, t)
                low = low + e
    return two_sum(h, low)


def local_kernel(corpus_ref, sketch_ref, sample_ref, mine_ref, other_ref, k0_ref, k1_ref, k2_ref, s_ref, x_ref):
    step = pl.program_id(0)

    @pl.when(step == 0)
    def _():
        k0_ref[...], k1_ref[...], k2_ref[...] = split3(sketch_ref[...])
        x_ref[:, 512:] = jnp.zeros((256, 1024), F32)

    c0, c1, c2 = split3(corpus_ref[...])
    k0, k1, k2 = k0_ref[...], k1_ref[...], k2_ref[...]
    s = dot16(c0, k0) + ((dot16(c0, k1) + dot16(c1, k0)) + (dot16(c0, k2) + dot16(c1, k1) + dot16(c2, k0)))
    sample_ref[...] = s
    at = pl.multiple_of(step * ROWS_PER_STEP, ROWS_PER_STEP)
    s_ref[pl.ds(at, ROWS_PER_STEP), :] = s
    s0, s1, s2 = split3(s)
    tn = ((0,), (0,))
    w = dot16(s0, c0, tn) + (
        (dot16(s0, c1, tn) + dot16(s1, c0, tn)) + (dot16(s0, c2, tn) + dot16(s1, c1, tn) + dot16(s2, c0, tn))
    )
    x_ref[:, 512:] = x_ref[:, 512:] + w

    @pl.when(step == pl.num_programs(0) - 1)
    def _():
        top = jnp.max(jnp.abs(s_ref[...]), axis=0, keepdims=True)
        h, l = half_gram(s_ref, top, 1024)
        hi, e = two_sum(h, h.T)
        hi, lo = two_sum(hi, (l + l.T) + e)
        x_ref[:, :256] = hi
        x_ref[:, 256:512] = lo
        core = lax.axis_index(CORE)
        mine_ref[...] = x_ref[pl.ds(pl.multiple_of(core * 128, 128), 128), :]
        other_ref[...] = x_ref[pl.ds(pl.multiple_of((1 - core) * 128, 128), 128), :]


def local_terms(corpus, sketch):
    rows, width = corpus.shape
    cols = sketch.shape[1]
    half = jax.ShapeDtypeStruct((128, 1536), F32)
    return pl.pallas_call(
        local_kernel,
        grid=(rows // ROWS_PER_STEP,),
        in_specs=[
            pl.BlockSpec((ROWS_PER_STEP, width), lambda i: (i, 0)),
            pl.BlockSpec((width, cols), lambda i: (0, 0)),
        ],
        out_specs=[
            pl.BlockSpec((ROWS_PER_STEP, cols), lambda i: (i, 0)),
            pl.BlockSpec((128, 1536), lambda i: (0, 0)),
            pl.BlockSpec((128, 1536), lambda i: (0, 0)),
        ],
        out_shape=[jax.ShapeDtypeStruct((rows, cols), F32), half, half],
        scratch_shapes=[pltpu.VMEM((width, cols), BF16)] * 3
        + [pltpu.VMEM((rows, cols), F32), pltpu.VMEM((256, 1536), F32)],
        name="local_terms",
    )(corpus, sketch)


def added(parts):
    hi, lo, w = parts[0][:, :256], parts[0][:, 256:512], parts[0][:, 512:]
    for p in parts[1:]:
        hi, e = two_sum(hi, p[:, :256])
        lo = lo + (p[:, 256:512] + e)
        w = w + p[:, 512:]
    hi, lo = two_sum(hi, lo)
    return hi, lo, w


def pair_kernel(a_ref, b_ref, out_ref):
    out_ref[:, :256], out_ref[:, 256:512], out_ref[:, 512:] = added([a_ref[...], b_ref[...]])


def pair_sum(a, b):
    return pl.pallas_call(pair_kernel, out_shape=jax.ShapeDtypeStruct(a.shape, F32), name="pair_sum")(a, b)


def stack_kernel(x_ref, out_ref):
    hi, lo, w = added([x_ref[i] for i in range(x_ref.shape[0])])
    for i in range(out_ref.shape[0]):
        out_ref[i, :, :256], out_ref[i, :, 256:512], out_ref[i, :, 512:] = hi, lo, w


def stack_sum(x, copies):
    return pl.pallas_call(
        stack_kernel, out_shape=jax.ShapeDtypeStruct((copies, *x.shape[1:]), F32), name="stack_sum"
    )(x)


def block_inverse(d):
    b = d.shape[0]
    shape = (8, 2 * b)
    row, col = (lax.broadcasted_iota(jnp.int32, (b, b), i) for i in (0, 1))
    m = jnp.concatenate([d, (row == col).astype(F32)], axis=1)
    nt = b // 8
    tiles = [m[8 * t : 8 * t + 8] for t in range(nt)]
    sub = lax.broadcasted_iota(jnp.int32, shape, 0)
    for t in range(nt):
        u = [jnp.broadcast_to(tiles[t][i : i + 1, :], shape) for i in range(8)]
        s = {
            (i, j): jnp.broadcast_to(u[i][:, 8 * t + j : 8 * t + j + 1], shape) for i in range(8) for j in range(i, 8)
        }
        l, rho = {}, []
        for k in range(8):
            rho.append(lax.rsqrt(s[k, k]))
            for i in range(k + 1, 8):
                l[i, k] = s[k, i] * rho[k]
            for i in range(k + 1, 8):
                for j in range(i, 8):
                    s[i, j] = s[i, j] - l[i, k] * l[j, k]
            u[k] = u[k] * rho[k]
            for i in range(k + 1, 8):
                u[i] = u[i] - l[i, k] * u[k]
        out = u[0]
        for k in range(1, 8):
            out = jnp.where(sub == k, u[k], out)
        if t + 1 < nt:
            z = list(u)
            for k in range(7, -1, -1):
                z[k] = z[k] * rho[k]
                for i in range(k):
                    z[i] = z[i] - l[k, i] * z[k]
            for v in range(t + 1, nt):
                p = [jnp.broadcast_to(tiles[v][:, 8 * t + k : 8 * t + k + 1], shape) * z[k] for k in range(8)]
                while len(p) > 1:
                    p = [p[i] + p[i + 1] for i in range(0, len(p), 2)]
                tiles[v] = tiles[v] - p[0]
        tiles[t] = out
    return jnp.concatenate(tiles, axis=0)[:, b:]


def factor_kernel(root, near_ref, far_ref, inverse_ref, projection_ref, g_ref, w_ref, r_ref, y_ref, a_ref, m_ref, u_ref):
    n = 256
    core = lax.axis_index(CORE)
    for ref, half in ((near_ref, core), (far_ref, 1 - core)):
        at = pl.multiple_of(half * 128, 128)
        g_ref[pl.ds(at, 128), :] = ref[:, :512]
        w_ref[pl.ds(at, 128), :] = ref[:, 512:]
    row, col = (lax.broadcasted_iota(jnp.int32, (n, n), i) for i in (0, 1))
    eye = (row == col).astype(F32)
    lower = jnp.where(row > col, 1.0, jnp.where(row == col, 0.5, 0.0))

    a_ref[:, :n] = g_ref[:, :n]
    a_ref[:, n:] = eye
    r_ref[...] = jnp.zeros((n, n), F32)
    for lo in range(0, n, BLOCK):
        hi = lo + BLOCK
        p = dot(block_inverse(a_ref[lo:hi, lo:hi]), a_ref[lo:hi, :])
        r_ref[lo:hi, :] = p[:, :n]
        y_ref[lo:hi, :] = p[:, n:]
        if hi < n:
            a_ref[hi:, :] = a_ref[hi:, :] - dot(p[:, hi:n], p, ((0,), (0,)))
    r = jnp.where(row <= col, r_ref[...], 0.0)
    y = y_ref[...]

    tn, nt = ((0,), (0,)), ((1,), (1,))
    a = grid_slices(r, jnp.max(jnp.abs(r), axis=0, keepdims=True))
    both = lambda i, j: dot16(a[i], a[j], tn) + dot16(a[j], a[i], tn)
    d, e1 = two_sum(g_ref[:, :n], -dot16(a[0], a[0], tn))
    d, e2 = two_sum(d, -both(0, 1))
    fine = both(0, 2) + dot16(a[1], a[1], tn) + ((both(0, 3) + both(1, 2)) + (both(1, 3) + dot16(a[2], a[2], tn)))
    d = d + ((g_ref[:, n:] - fine) + (e1 + e2))

    f = dot(r, y, nt) - eye
    m = eye + ((f + f.T) + dot(f, f, tn) + dot(dot(y, d), y, nt))
    m_ref[...] = m
    u_ref[...] = eye - lower * (m - eye)

    def refine(carry):
        count, _ = carry
        u = u_ref[...]
        off = dot(dot(u, m_ref[...]), u, nt) - eye
        u_ref[...] = u - dot(lower * off, u)
        return count + 1, jnp.max(jnp.abs(off))

    lax.while_loop(lambda c: (c[0] < 24) & (c[1] > 1e-4), refine, (0, jnp.float32(1.0)))
    y = dot(u_ref[...], y)
    inverse_ref[...] = y * root
    projection_ref[...] = dot(y * (1.0 / root), w_ref[...])


def factored(near, far, root):
    import functools

    n = 256
    return pl.pallas_call(
        functools.partial(factor_kernel, root),
        out_shape=[jax.ShapeDtypeStruct((n, n), F32), jax.ShapeDtypeStruct((n, 1024), F32)],
        scratch_shapes=[
            pltpu.VMEM(s, F32) for s in ((n, 512), (n, 1024), (n, n), (n, n), (n, 512), (n, n), (n, n))
        ],
        name="factored",
    )(near, far)


def exchanged(x, axis):
    return lax.all_to_all(x, axis, 0, 0, tiled=True)


def on_device(corpus, sketch):
    plane, line = lax.axis_size(PLANE), lax.axis_size(LINE)
    total_rows = corpus.shape[0] * plane * line * lax.axis_size(CORE)
    root = math.sqrt(total_rows)
    swap = [(0, 1), (1, 0)]
    sample, mine, other = local_terms(corpus, sketch)
    own = pair_sum(mine, lax.ppermute(other, CORE, swap))
    piece = stack_sum(exchanged(own.reshape(plane, 8, 1536), PLANE), line)
    whole = stack_sum(exchanged(piece, LINE), plane)
    near = exchanged(whole, PLANE).reshape(128, 1536)
    far = lax.ppermute(near, CORE, swap)
    inverse, projection = factored(near, far, root)
    basis = dot(sample, inverse, ((1,), (1,)))
    return (basis, projection)


def solution(mesh):
    finer = Mesh(
        mesh.devices.reshape(4, 4, 2, mesh.shape["narrow"]),
        ("wide_0", "wide_1", "wide_2", "narrow"),
    )
    in_specs = (P(WIDE_NARROW, None), P())
    out_specs = (P(WIDE_NARROW, None), P())
    return jax.shard_map(on_device, mesh=finer, in_specs=in_specs, out_specs=out_specs, check_vma=False)
```

```python
import functools
import math

import jax
import jax.numpy as jnp
from jax import lax
from jax.experimental import pallas as pl
from jax.experimental.pallas import tpu as pltpu
from jax.sharding import Mesh
from jax.sharding import PartitionSpec as P

WIDE_NARROW = ("wide_0", "wide_1", "wide_2", "narrow")
PLANE = ("wide_0", "wide_1")
CORE = "wide_2"
LINE = "narrow"
HI = lax.Precision.HIGHEST
F32 = jnp.float32
BF16 = jnp.bfloat16
BLOCK = 64


def dot(a, b, dims=((1,), (0,)), precision=HI):
    return lax.dot_general(a, b, (dims, ((), ())), precision=precision, preferred_element_type=F32)


def dot16(a, b, dims=((1,), (0,))):
    return lax.dot_general(a, b, (dims, ((), ())), preferred_element_type=F32)


def two_sum(a, b):
    s = a + b
    t = s - a
    return s, (a - (s - t)) + (b - t)


def grid_slices(x, top):
    out = []
    for i in range(4):
        edge = top * (2.0 ** (17 - 8 * i))
        a = (x + edge) - edge
        out.append(a.astype(BF16))
        x = x - a
    return out


def half_gram(s, top, rows):
    tn = ((0,), (0,))
    h = l = low = None
    for at in range(0, s.shape[0], rows):
        a = grid_slices(s[at : at + rows, :], top)
        terms = [0.5 * dot16(a[0], a[0], tn), dot16(a[0], a[1], tn)]
        rest = (dot16(a[0], a[2], tn) + 0.5 * dot16(a[1], a[1], tn)) + (
            (dot16(a[0], a[3], tn) + dot16(a[1], a[2], tn)) + (dot16(a[1], a[3], tn) + 0.5 * dot16(a[2], a[2], tn))
        )
        low = rest if low is None else low + rest
        for t in terms:
            if h is None:
                h = t
            else:
                h, e = two_sum(h, t)
                low = low + e
    return two_sum(h, low)


def in_vmem(n):
    return [pl.BlockSpec(memory_space=pltpu.VMEM)] * n


def gram_kernel(sample_ref, terms_ref, mine_ref, other_ref, x_ref):
    top = jnp.max(jnp.abs(sample_ref[...]), axis=0, keepdims=True)
    h, l = half_gram(sample_ref, top, 1024)
    hi, e = two_sum(h, h.T)
    hi, lo = two_sum(hi, (l + l.T) + e)
    x_ref[:, :256] = hi
    x_ref[:, 256:] = lo
    core = lax.axis_index(CORE)
    for half, ref in ((core, mine_ref), (1 - core, other_ref)):
        at = pl.multiple_of(half * 128, 128)
        ref[:, :512] = x_ref[pl.ds(at, 128), :]
        ref[:, 512:] = terms_ref[pl.ds(at, 128), :]


def local_halves(sample, terms):
    return pl.pallas_call(
        gram_kernel,
        in_specs=in_vmem(2),
        out_specs=in_vmem(2),
        out_shape=[jax.ShapeDtypeStruct((128, 1536), F32)] * 2,
        scratch_shapes=[pltpu.VMEM((256, 512), F32)],
        compiler_params=pltpu.CompilerParams(vmem_limit_bytes=20 * 2**20),
        name="local_halves",
    )(sample, terms)


def added(parts):
    hi, lo, w = parts[0][:, :256], parts[0][:, 256:512], parts[0][:, 512:]
    for p in parts[1:]:
        hi, e = two_sum(hi, p[:, :256])
        lo = lo + (p[:, 256:512] + e)
        w = w + p[:, 512:]
    hi, lo = two_sum(hi, lo)
    return hi, lo, w


def pair_kernel(a_ref, b_ref, out_ref):
    out_ref[:, :256], out_ref[:, 256:512], out_ref[:, 512:] = added([a_ref[...], b_ref[...]])


def pair_sum(a, b):
    return pl.pallas_call(
        pair_kernel,
        in_specs=in_vmem(2),
        out_specs=in_vmem(1)[0],
        out_shape=jax.ShapeDtypeStruct(a.shape, F32),
        compiler_params=pltpu.CompilerParams(vmem_limit_bytes=6 * 2**20),
        name="pair_sum",
    )(a, b)


def stack_kernel(x_ref, out_ref):
    hi, lo, w = added([x_ref[i] for i in range(x_ref.shape[0])])
    for i in range(out_ref.shape[0]):
        out_ref[i, :, :256], out_ref[i, :, 256:512], out_ref[i, :, 512:] = hi, lo, w


def stack_sum(x, copies):
    return pl.pallas_call(
        stack_kernel,
        in_specs=in_vmem(1),
        out_specs=in_vmem(1)[0],
        out_shape=jax.ShapeDtypeStruct((copies, *x.shape[1:]), F32),
        compiler_params=pltpu.CompilerParams(vmem_limit_bytes=6 * 2**20),
        name="stack_sum",
    )(x)


def block_inverse(d):
    b = d.shape[0]
    shape = (8, 2 * b)
    row, col = (lax.broadcasted_iota(jnp.int32, (b, b), i) for i in (0, 1))
    m = jnp.concatenate([d, (row == col).astype(F32)], axis=1)
    nt = b // 8
    tiles = [m[8 * t : 8 * t + 8] for t in range(nt)]
    sub = lax.broadcasted_iota(jnp.int32, shape, 0)
    for t in range(nt):
        u = [jnp.broadcast_to(tiles[t][i : i + 1, :], shape) for i in range(8)]
        s = {
            (i, j): jnp.broadcast_to(u[i][:, 8 * t + j : 8 * t + j + 1], shape) for i in range(8) for j in range(i, 8)
        }
        l, rho = {}, []
        for k in range(8):
            rho.append(lax.rsqrt(s[k, k]))
            for i in range(k + 1, 8):
                l[i, k] = s[k, i] * rho[k]
            for i in range(k + 1, 8):
                for j in range(i, 8):
                    s[i, j] = s[i, j] - l[i, k] * l[j, k]
            u[k] = u[k] * rho[k]
            for i in range(k + 1, 8):
                u[i] = u[i] - l[i, k] * u[k]
        out = u[0]
        for k in range(1, 8):
            out = jnp.where(sub == k, u[k], out)
        if t + 1 < nt:
            z = list(u)
            for k in range(7, -1, -1):
                z[k] = z[k] * rho[k]
                for i in range(k):
                    z[i] = z[i] - l[k, i] * z[k]
            for v in range(t + 1, nt):
                p = [jnp.broadcast_to(tiles[v][:, 8 * t + k : 8 * t + k + 1], shape) * z[k] for k in range(8)]
                while len(p) > 1:
                    p = [p[i] + p[i + 1] for i in range(0, len(p), 2)]
                tiles[v] = tiles[v] - p[0]
        tiles[t] = out
    return jnp.concatenate(tiles, axis=0)[:, b:]


def factor_kernel(root, near_ref, far_ref, inverse_ref, projection_ref, g_ref, w_ref, r_ref, y_ref, a_ref, m_ref, u_ref):
    n = 256
    core = lax.axis_index(CORE)
    for ref, half in ((near_ref, core), (far_ref, 1 - core)):
        at = pl.multiple_of(half * 128, 128)
        g_ref[pl.ds(at, 128), :] = ref[:, :512]
        w_ref[pl.ds(at, 128), :] = ref[:, 512:]
    row, col = (lax.broadcasted_iota(jnp.int32, (n, n), i) for i in (0, 1))
    eye = (row == col).astype(F32)
    lower = jnp.where(row > col, 1.0, jnp.where(row == col, 0.5, 0.0))

    a_ref[:, :n] = g_ref[:, :n]
    a_ref[:, n:] = eye
    r_ref[...] = jnp.zeros((n, n), F32)
    for lo in range(0, n, BLOCK):
        hi = lo + BLOCK
        p = dot(block_inverse(a_ref[lo:hi, lo:hi]), a_ref[lo:hi, :])
        r_ref[lo:hi, :] = p[:, :n]
        y_ref[lo:hi, :] = p[:, n:]
        if hi < n:
            a_ref[hi:, :] = a_ref[hi:, :] - dot(p[:, hi:n], p, ((0,), (0,)))
    r = jnp.where(row <= col, r_ref[...], 0.0)
    y = y_ref[...]

    tn, nt = ((0,), (0,)), ((1,), (1,))
    a = grid_slices(r, jnp.max(jnp.abs(r), axis=0, keepdims=True))
    both = lambda i, j: dot16(a[i], a[j], tn) + dot16(a[j], a[i], tn)
    d, e1 = two_sum(g_ref[:, :n], -dot16(a[0], a[0], tn))
    d, e2 = two_sum(d, -both(0, 1))
    fine = both(0, 2) + dot16(a[1], a[1], tn) + ((both(0, 3) + both(1, 2)) + (both(1, 3) + dot16(a[2], a[2], tn)))
    d = d + ((g_ref[:, n:] - fine) + (e1 + e2))

    f = dot(r, y, nt) - eye
    m = eye + ((f + f.T) + dot(f, f, tn) + dot(dot(y, d), y, nt))
    m_ref[...] = m
    u_ref[...] = eye - lower * (m - eye)

    def refine(carry):
        count, _ = carry
        u = u_ref[...]
        off = dot(dot(u, m_ref[...]), u, nt) - eye
        u_ref[...] = u - dot(lower * off, u)
        return count + 1, jnp.max(jnp.abs(off))

    lax.while_loop(lambda c: (c[0] < 24) & (c[1] > 1e-4), refine, (0, jnp.float32(1.0)))
    y = dot(u_ref[...], y)
    inverse_ref[...] = (y * root).T
    projection_ref[...] = dot(y * (1.0 / root), w_ref[...])


def factored(near, far, root):
    n = 256
    return pl.pallas_call(
        functools.partial(factor_kernel, root),
        in_specs=in_vmem(2),
        out_specs=in_vmem(2),
        out_shape=[jax.ShapeDtypeStruct((n, n), F32), jax.ShapeDtypeStruct((n, 1024), F32)],
        scratch_shapes=[
            pltpu.VMEM(s, F32) for s in ((n, 512), (n, 1024), (n, n), (n, n), (n, 512), (n, n), (n, n))
        ],
        compiler_params=pltpu.CompilerParams(vmem_limit_bytes=16 * 2**20),
        name="factored",
    )(near, far)


def exchanged(x, axis):
    return lax.all_to_all(x, axis, 0, 0, tiled=True)


def on_device(corpus, sketch):
    plane, line = lax.axis_size(PLANE), lax.axis_size(LINE)
    total_rows = corpus.shape[0] * plane * line * lax.axis_size(CORE)
    root = math.sqrt(total_rows)
    swap = [(0, 1), (1, 0)]
    sample = dot(corpus, sketch)
    terms = dot(sample, corpus, ((0,), (0,)), lax.Precision.HIGH)
    mine, other = local_halves(sample, terms)
    own = pair_sum(mine, lax.ppermute(other, CORE, swap))
    piece = stack_sum(exchanged(own.reshape(plane, 8, 1536), PLANE), line)
    whole = stack_sum(exchanged(piece, LINE), plane)
    near = exchanged(whole, PLANE).reshape(128, 1536)
    far = lax.ppermute(near, CORE, swap)
    inverse, projection = factored(near, far, root)
    basis = dot(sample, inverse)
    return (basis, projection)


def solution(mesh):
    finer = Mesh(
        mesh.devices.reshape(4, 4, 2, mesh.shape["narrow"]),
        ("wide_0", "wide_1", "wide_2", "narrow"),
    )
    in_specs = (P(WIDE_NARROW, None), P())
    out_specs = (P(WIDE_NARROW, None), P())
    return jax.shard_map(on_device, mesh=finer, in_specs=in_specs, out_specs=out_specs, check_vma=False)
```

```python
import functools
import math

import jax
import jax.numpy as jnp
from jax import lax
from jax.experimental import pallas as pl
from jax.experimental.pallas import tpu as pltpu
from jax.sharding import Mesh
from jax.sharding import PartitionSpec as P

WIDE_NARROW = ("wide_0", "wide_1", "wide_2", "narrow")
PLANE = ("wide_0", "wide_1")
CORE = "wide_2"
LINE = "narrow"
HI = lax.Precision.HIGHEST
F32 = jnp.float32
BF16 = jnp.bfloat16
BLOCK = 64


def dot(a, b, dims=((1,), (0,)), precision=HI):
    return lax.dot_general(a, b, (dims, ((), ())), precision=precision, preferred_element_type=F32)


def dot16(a, b, dims=((1,), (0,))):
    return lax.dot_general(a, b, (dims, ((), ())), preferred_element_type=F32)


def two_sum(a, b):
    s = a + b
    t = s - a
    return s, (a - (s - t)) + (b - t)


def grid_slices(x, top):
    out = []
    for i in range(4):
        edge = top * (2.0 ** (17 - 8 * i))
        a = (x + edge) - edge
        out.append(a.astype(BF16))
        x = x - a
    return out


def half_gram(s, top, rows):
    tn = ((0,), (0,))
    h = l = low = None
    for at in range(0, s.shape[0], rows):
        a = grid_slices(s[at : at + rows, :], top)
        terms = [0.5 * dot16(a[0], a[0], tn), dot16(a[0], a[1], tn)]
        rest = (dot16(a[0], a[2], tn) + 0.5 * dot16(a[1], a[1], tn)) + (
            (dot16(a[0], a[3], tn) + dot16(a[1], a[2], tn)) + (dot16(a[1], a[3], tn) + 0.5 * dot16(a[2], a[2], tn))
        )
        low = rest if low is None else low + rest
        for t in terms:
            if h is None:
                h = t
            else:
                h, e = two_sum(h, t)
                low = low + e
    return two_sum(h, low)


def in_vmem(n):
    return [pl.BlockSpec(memory_space=pltpu.VMEM)] * n


def gram_kernel(sample_ref, terms_ref, mine_ref, other_ref, x_ref):
    top = jnp.max(jnp.abs(sample_ref[...]), axis=0, keepdims=True)
    h, l = half_gram(sample_ref, top, 1024)
    hi, e = two_sum(h, h.T)
    hi, lo = two_sum(hi, (l + l.T) + e)
    x_ref[:, :256] = hi
    x_ref[:, 256:] = lo
    core = lax.axis_index(CORE)
    for half, ref in ((core, mine_ref), (1 - core, other_ref)):
        at = pl.multiple_of(half * 128, 128)
        ref[:, :512] = x_ref[pl.ds(at, 128), :]
        ref[:, 512:] = terms_ref[pl.ds(at, 128), :]


def local_halves(sample, terms):
    return pl.pallas_call(
        gram_kernel,
        in_specs=in_vmem(2),
        out_specs=in_vmem(2),
        out_shape=[jax.ShapeDtypeStruct((128, 1536), F32)] * 2,
        scratch_shapes=[pltpu.VMEM((256, 512), F32)],
        compiler_params=pltpu.CompilerParams(vmem_limit_bytes=20 * 2**20),
        name="local_halves",
    )(sample, terms)


def plus(a, b):
    hi, e = two_sum(a[:, :256], b[:, :256])
    hi, lo = two_sum(hi, (a[:, 256:512] + b[:, 256:512]) + e)
    return jnp.concatenate([hi, lo, a[:, 512:] + b[:, 512:]], axis=1)


def pair_kernel(a_ref, b_ref, out_ref):
    s = plus(a_ref[...], b_ref[...])
    if len(out_ref.shape) == 2:
        out_ref[...] = s
    else:
        for i in range(out_ref.shape[0]):
            out_ref[i] = s


def stack_kernel(x_ref, out_ref):
    parts = [x_ref[i] for i in range(x_ref.shape[0])]
    while len(parts) > 1:
        parts = [plus(parts[i], parts[i + 1]) for i in range(0, len(parts), 2)]
    out_ref[...] = parts[0]


def added(kernel, shape, name, *parts):
    return pl.pallas_call(
        kernel,
        in_specs=in_vmem(len(parts)),
        out_specs=in_vmem(1)[0],
        out_shape=jax.ShapeDtypeStruct(shape, F32),
        compiler_params=pltpu.CompilerParams(vmem_limit_bytes=6 * 2**20),
        name=name,
    )(*parts)


def block_inverse(d):
    b = d.shape[0]
    shape = (8, 2 * b)
    row, col = (lax.broadcasted_iota(jnp.int32, (b, b), i) for i in (0, 1))
    m = jnp.concatenate([d, (row == col).astype(F32)], axis=1)
    nt = b // 8
    tiles = [m[8 * t : 8 * t + 8] for t in range(nt)]
    sub = lax.broadcasted_iota(jnp.int32, shape, 0)
    for t in range(nt):
        across = lambda x, j: jnp.broadcast_to(x[:, 8 * t + j : 8 * t + j + 1], shape)
        u = [jnp.broadcast_to(tiles[t][i : i + 1, :], shape) for i in range(8)]
        s = {(i, j): across(u[i], j) for i in range(8) for j in range(i, 8)}
        below = {v: [across(tiles[v], k) for k in range(8)] for v in range(t + 1, nt)}
        l = {}
        for k in range(8):
            rho = lax.rsqrt(s[k, k])
            for i in range(k + 1, 8):
                l[i] = s[k, i] * rho
            for i in range(k + 1, 8):
                for j in range(i, 8):
                    s[i, j] = s[i, j] - l[i] * l[j]
            for w in [u, *below.values()]:
                w[k] = w[k] * rho
                for i in range(k + 1, 8):
                    w[i] = w[i] - l[i] * w[k]
        out = u[0]
        for k in range(1, 8):
            out = jnp.where(sub == k, u[k], out)
        for v, w in below.items():
            p = [w[k] * u[k] for k in range(8)]
            while len(p) > 1:
                p = [p[i] + p[i + 1] for i in range(0, len(p), 2)]
            tiles[v] = tiles[v] - p[0]
        tiles[t] = out
    return jnp.concatenate(tiles, axis=0)[:, b:]


def factor_kernel(root, near_ref, far_ref, inverse_ref, projection_ref, g_ref, w_ref, r_ref, y_ref, a_ref, m_ref, u_ref):
    n = 256
    core = lax.axis_index(CORE)
    for ref, half in ((near_ref, core), (far_ref, 1 - core)):
        at = pl.multiple_of(half * 128, 128)
        g_ref[pl.ds(at, 128), :] = ref[:, :512]
        w_ref[pl.ds(at, 128), :] = ref[:, 512:]
    row, col = (lax.broadcasted_iota(jnp.int32, (n, n), i) for i in (0, 1))
    eye = (row == col).astype(F32)
    lower = jnp.where(row > col, 1.0, jnp.where(row == col, 0.5, 0.0))

    a_ref[:, :n] = g_ref[:, :n]
    a_ref[:, n:] = eye
    r_ref[...] = jnp.zeros((n, n), F32)
    for lo in range(0, n, BLOCK):
        hi = lo + BLOCK
        p = dot(block_inverse(a_ref[lo:hi, lo:hi]), a_ref[lo:hi, :])
        r_ref[lo:hi, :] = p[:, :n]
        y_ref[lo:hi, :] = p[:, n:]
        if hi < n:
            a_ref[hi:, :] = a_ref[hi:, :] - dot(p[:, hi:n], p, ((0,), (0,)))
    r = jnp.where(row <= col, r_ref[...], 0.0)
    y = y_ref[...]

    tn, nt = ((0,), (0,)), ((1,), (1,))
    a = grid_slices(r, jnp.max(jnp.abs(r), axis=0, keepdims=True))
    both = lambda i, j: dot16(a[i], a[j], tn) + dot16(a[j], a[i], tn)
    d, e1 = two_sum(g_ref[:, :n], -dot16(a[0], a[0], tn))
    d, e2 = two_sum(d, -both(0, 1))
    fine = both(0, 2) + dot16(a[1], a[1], tn) + ((both(0, 3) + both(1, 2)) + (both(1, 3) + dot16(a[2], a[2], tn)))
    d = d + ((g_ref[:, n:] - fine) + (e1 + e2))

    f = dot(r, y, nt) - eye
    m = eye + ((f + f.T) + dot(f, f, tn) + dot(dot(y, d), y, nt))
    m_ref[...] = m
    u_ref[...] = eye - lower * (m - eye)

    def refine(carry):
        count, _ = carry
        u = u_ref[...]
        off = dot(dot(u, m_ref[...]), u, nt) - eye
        u_ref[...] = u - dot(lower * off, u)
        return count + 1, jnp.max(jnp.abs(off))

    lax.while_loop(lambda c: (c[0] < 24) & (c[1] > 1e-4), refine, (0, jnp.float32(1.0)))
    y = dot(u_ref[...], y)
    inverse_ref[...] = (y * root).T
    projection_ref[...] = dot(y * (1.0 / root), w_ref[...])


def factored(near, far, root):
    n = 256
    return pl.pallas_call(
        functools.partial(factor_kernel, root),
        in_specs=in_vmem(2),
        out_specs=in_vmem(2),
        out_shape=[jax.ShapeDtypeStruct((n, n), F32), jax.ShapeDtypeStruct((n, 1024), F32)],
        scratch_shapes=[
            pltpu.VMEM(s, F32) for s in ((n, 512), (n, 1024), (n, n), (n, n), (n, 512), (n, n), (n, n))
        ],
        compiler_params=pltpu.CompilerParams(vmem_limit_bytes=16 * 2**20),
        name="factored",
    )(near, far)


def exchanged(x, axis):
    return lax.all_to_all(x, axis, 0, 0, tiled=True)


def on_device(corpus, sketch):
    plane, line = lax.axis_size(PLANE), lax.axis_size(LINE)
    total_rows = corpus.shape[0] * plane * line * lax.axis_size(CORE)
    root = math.sqrt(total_rows)
    swap = [(0, 1), (1, 0)]
    sample = dot(corpus, sketch)
    terms = dot(sample, corpus, ((0,), (0,)), lax.Precision.HIGH)
    mine, other = local_halves(sample, terms)
    own = added(pair_kernel, mine.shape, "pair_sum", mine, lax.ppermute(other, CORE, swap))
    whole = added(stack_kernel, (8, 1536), "stack_sum", exchanged(own.reshape(plane, 8, 1536), PLANE))
    far = 1
    while far < line:
        arrived = lax.ppermute(whole, LINE, [(i, i ^ far) for i in range(line)])
        far *= 2
        out = (8, 1536) if far < line else (plane, 8, 1536)
        whole = added(pair_kernel, out, "pair_sum", whole, arrived)
    near = exchanged(whole, PLANE).reshape(128, 1536)
    far = lax.ppermute(near, CORE, swap)
    inverse, projection = factored(near, far, root)
    basis = dot(sample, inverse)
    return (basis, projection)


def solution(mesh):
    finer = Mesh(
        mesh.devices.reshape(4, 4, 2, mesh.shape["narrow"]),
        ("wide_0", "wide_1", "wide_2", "narrow"),
    )
    in_specs = (P(WIDE_NARROW, None), P())
    out_specs = (P(WIDE_NARROW, None), P())
    return jax.shard_map(on_device, mesh=finer, in_specs=in_specs, out_specs=out_specs, check_vma=False)
```

```python
import functools
import math

import jax
import jax.numpy as jnp
from jax import lax
from jax.experimental import pallas as pl
from jax.experimental.pallas import tpu as pltpu
from jax.sharding import Mesh
from jax.sharding import PartitionSpec as P

WIDE_NARROW = ("wide_0", "wide_1", "wide_2", "narrow")
PLANE = ("wide_0", "wide_1")
CORE = "wide_2"
LINE = "narrow"
HI = lax.Precision.HIGHEST
F32 = jnp.float32
BF16 = jnp.bfloat16
BLOCK = 128
GRAM = 384
WIDTH = GRAM + 1024


def dot(a, b, dims=((1,), (0,)), precision=HI):
    return lax.dot_general(a, b, (dims, ((), ())), precision=precision, preferred_element_type=F32)


def dot16(a, b, dims=((1,), (0,))):
    return lax.dot_general(a, b, (dims, ((), ())), preferred_element_type=F32)


def two_sum(a, b):
    s = a + b
    t = s - a
    return s, (a - (s - t)) + (b - t)


def grid_slices(x, top):
    out = []
    for i in range(4):
        edge = top * (2.0 ** (17 - 8 * i))
        a = (x + edge) - edge
        out.append(a.astype(BF16))
        x = x - a
    return out


def half_gram(s, top, rows):
    tn = ((0,), (0,))
    h = l = low = None
    for at in range(0, s.shape[0], rows):
        a = grid_slices(s[at : at + rows, :], top)
        terms = [0.5 * dot16(a[0], a[0], tn), dot16(a[0], a[1], tn)]
        rest = (dot16(a[0], a[2], tn) + 0.5 * dot16(a[1], a[1], tn)) + (
            (dot16(a[0], a[3], tn) + dot16(a[1], a[2], tn)) + (dot16(a[1], a[3], tn) + 0.5 * dot16(a[2], a[2], tn))
        )
        low = rest if low is None else low + rest
        for t in terms:
            if h is None:
                h = t
            else:
                h, e = two_sum(h, t)
                low = low + e
    return two_sum(h, low)


def in_vmem(n):
    return [pl.BlockSpec(memory_space=pltpu.VMEM)] * n


def gram_kernel(sample_ref, terms_ref, mine_ref, other_ref, x_ref):
    top = jnp.max(jnp.abs(sample_ref[...]), axis=0, keepdims=True)
    h, l = half_gram(sample_ref, top, 1024)
    hi, e = two_sum(h, h.T)
    hi, lo = two_sum(hi, (l + l.T) + e)
    for i in range(2):
        at, mid = 128 * i, 128 + 64 * i
        x_ref[i, :, :128] = hi[at : at + 128, at : at + 128]
        x_ref[i, :, 128:256] = lo[at : at + 128, at : at + 128]
        x_ref[i, :, 256:320] = hi[:128, mid : mid + 64]
        x_ref[i, :, 320:] = lo[:128, mid : mid + 64]
    core = lax.axis_index(CORE)
    for half, ref in ((core, mine_ref), (1 - core, other_ref)):
        ref[:, :GRAM] = x_ref[half]
        ref[:, GRAM:] = terms_ref[pl.ds(pl.multiple_of(half * 128, 128), 128), :]


def local_halves(sample, terms):
    return pl.pallas_call(
        gram_kernel,
        in_specs=in_vmem(2),
        out_specs=in_vmem(2),
        out_shape=[jax.ShapeDtypeStruct((128, WIDTH), F32)] * 2,
        scratch_shapes=[pltpu.VMEM((2, 128, GRAM), F32)],
        compiler_params=pltpu.CompilerParams(vmem_limit_bytes=20 * 2**20),
        name="local_halves",
    )(sample, terms)


def plus(a, b):
    out = []
    for at, w in ((0, 128), (256, 64)):
        hi, e = two_sum(a[:, at : at + w], b[:, at : at + w])
        low = slice(at + w, at + 2 * w)
        out += two_sum(hi, (a[:, low] + b[:, low]) + e)
    return jnp.concatenate([*out, a[:, GRAM:] + b[:, GRAM:]], axis=1)


def pair_kernel(a_ref, b_ref, out_ref):
    s = plus(a_ref[...], b_ref[...])
    if len(out_ref.shape) == 2:
        out_ref[...] = s
    else:
        for i in range(out_ref.shape[0]):
            out_ref[i] = s


def stack_kernel(x_ref, out_ref):
    parts = [x_ref[i] for i in range(x_ref.shape[0])]
    while len(parts) > 1:
        parts = [plus(parts[i], parts[i + 1]) for i in range(0, len(parts), 2)]
    out_ref[...] = parts[0]


def added(kernel, shape, name, *parts):
    return pl.pallas_call(
        kernel,
        in_specs=in_vmem(len(parts)),
        out_specs=in_vmem(1)[0],
        out_shape=jax.ShapeDtypeStruct(shape, F32),
        compiler_params=pltpu.CompilerParams(vmem_limit_bytes=6 * 2**20),
        name=name,
    )(*parts)


def block_inverse(d):
    b = d.shape[0]
    shape = (8, 2 * b)
    row, col = (lax.broadcasted_iota(jnp.int32, (b, b), i) for i in (0, 1))
    m = jnp.concatenate([d, (row == col).astype(F32)], axis=1)
    nt = b // 8
    tiles = [m[8 * t : 8 * t + 8] for t in range(nt)]
    sub = lax.broadcasted_iota(jnp.int32, shape, 0)
    for t in range(nt):
        across = lambda x, j: jnp.broadcast_to(x[:, 8 * t + j : 8 * t + j + 1], shape)
        u = [jnp.broadcast_to(tiles[t][i : i + 1, :], shape) for i in range(8)]
        s = {(i, j): across(u[i], j) for i in range(8) for j in range(i, 8)}
        near = {v: [across(tiles[v], k) for k in range(8)] for v in range(t + 1, min(t + 2, nt))}
        l, scale = {}, []
        for k in range(8):
            rho = lax.rsqrt(s[k, k])
            scale.append(rho)
            for i in range(k + 1, 8):
                l[i, k] = s[k, i] * rho
            for i in range(k + 1, 8):
                for j in range(i, 8):
                    s[i, j] = s[i, j] - l[i, k] * l[j, k]
            for w in [u, *near.values()]:
                w[k] = w[k] * rho
                for i in range(k + 1, 8):
                    w[i] = w[i] - l[i, k] * w[k]
        out = u[0]
        for k in range(1, 8):
            out = jnp.where(sub == k, u[k], out)
        z = list(u)
        if t + 2 < nt:
            for k in range(7, -1, -1):
                z[k] = z[k] * scale[k]
                for i in range(k):
                    z[i] = z[i] - l[k, i] * z[k]
        for v in range(t + 1, nt):
            if v in near:
                p = [near[v][k] * u[k] for k in range(8)]
            else:
                p = [across(tiles[v], k) * z[k] for k in range(8)]
            while len(p) > 1:
                p = [p[i] + p[i + 1] for i in range(0, len(p), 2)]
            tiles[v] = tiles[v] - p[0]
        tiles[t] = out
    return jnp.concatenate(tiles, axis=0)[:, b:]


def factor_kernel(root, near_ref, far_ref, inverse_ref, projection_ref, x_ref, g_ref, w_ref, r_ref, y_ref, a_ref, m_ref, u_ref):
    n = 256
    core = lax.axis_index(CORE)
    for ref, half in ((near_ref, core), (far_ref, 1 - core)):
        x_ref[half] = ref[:, :GRAM]
        w_ref[pl.ds(pl.multiple_of(half * 128, 128), 128), :] = ref[:, GRAM:]
    for at in (0, 1):
        corner = [x_ref[i, :, 128 * at : 128 * at + 128] for i in (0, 1)]
        side = jnp.concatenate([x_ref[i, :, 256 + 64 * at : 320 + 64 * at] for i in (0, 1)], axis=1)
        g_ref[:128, n * at : n * at + 128] = corner[0]
        g_ref[:128, n * at + 128 : n * at + n] = side
        g_ref[128:, n * at : n * at + 128] = side.T
        g_ref[128:, n * at + 128 : n * at + n] = corner[1]
    row, col = (lax.broadcasted_iota(jnp.int32, (n, n), i) for i in (0, 1))
    eye = (row == col).astype(F32)
    lower = jnp.where(row > col, 1.0, jnp.where(row == col, 0.5, 0.0))

    a_ref[:, :n] = g_ref[:, :n]
    a_ref[:, n:] = eye
    r_ref[...] = jnp.zeros((n, n), F32)
    for lo in range(0, n, BLOCK):
        hi = lo + BLOCK
        p = dot(block_inverse(a_ref[lo:hi, lo:hi]), a_ref[lo:hi, :])
        r_ref[lo:hi, :] = p[:, :n]
        y_ref[lo:hi, :] = p[:, n:]
        if hi < n:
            a_ref[hi:, :] = a_ref[hi:, :] - dot(p[:, hi:n], p, ((0,), (0,)))
    r = jnp.where(row <= col, r_ref[...], 0.0)
    y = y_ref[...]

    tn, nt = ((0,), (0,)), ((1,), (1,))
    a = grid_slices(r, jnp.max(jnp.abs(r), axis=0, keepdims=True))
    both = lambda i, j: dot16(a[i], a[j], tn) + dot16(a[j], a[i], tn)
    d, e1 = two_sum(g_ref[:, :n], -dot16(a[0], a[0], tn))
    d, e2 = two_sum(d, -both(0, 1))
    fine = both(0, 2) + dot16(a[1], a[1], tn) + ((both(0, 3) + both(1, 2)) + (both(1, 3) + dot16(a[2], a[2], tn)))
    d = d + ((g_ref[:, n:] - fine) + (e1 + e2))

    f = dot(r, y, nt) - eye
    m = eye + ((f + f.T) + dot(f, f, tn) + dot(dot(y, d), y, nt))
    m_ref[...] = m
    u_ref[...] = eye - lower * (m - eye)

    def refine(carry):
        count, _ = carry
        u = u_ref[...]
        off = dot(dot(u, m_ref[...]), u, nt) - eye
        u_ref[...] = u - dot(lower * off, u)
        return count + 1, jnp.max(jnp.abs(off))

    lax.while_loop(lambda c: (c[0] < 24) & (c[1] > 1e-4), refine, (0, jnp.float32(1.0)))
    y = dot(u_ref[...], y)
    inverse_ref[...] = (y * root).T
    projection_ref[...] = dot(y * (1.0 / root), w_ref[...])


def factored(near, far, root):
    n = 256
    return pl.pallas_call(
        functools.partial(factor_kernel, root),
        in_specs=in_vmem(2),
        out_specs=in_vmem(2),
        out_shape=[jax.ShapeDtypeStruct((n, n), F32), jax.ShapeDtypeStruct((n, 1024), F32)],
        scratch_shapes=[
            pltpu.VMEM(s, F32) for s in ((2, 128, GRAM), (n, 512), (n, 1024), (n, n), (n, n), (n, 512), (n, n), (n, n))
        ],
        compiler_params=pltpu.CompilerParams(vmem_limit_bytes=16 * 2**20),
        name="factored",
    )(near, far)


def exchanged(x, axis):
    return lax.all_to_all(x, axis, 0, 0, tiled=True)


def on_device(corpus, sketch):
    plane, line = lax.axis_size(PLANE), lax.axis_size(LINE)
    total_rows = corpus.shape[0] * plane * line * lax.axis_size(CORE)
    root = math.sqrt(total_rows)
    swap = [(0, 1), (1, 0)]
    sample = dot(corpus, sketch)
    terms = dot(sample, corpus, ((0,), (0,)), lax.Precision.HIGH)
    mine, other = local_halves(sample, terms)
    own = added(pair_kernel, mine.shape, "pair_sum", mine, lax.ppermute(other, CORE, swap))
    whole = added(stack_kernel, (8, WIDTH), "stack_sum", exchanged(own.reshape(plane, 8, WIDTH), PLANE))
    reach = 1
    while reach < line:
        flip = reach if 2 * reach < line else line - 1
        arrived = lax.ppermute(whole, LINE, [(i, i ^ flip) for i in range(line)])
        reach *= 2
        out = (8, WIDTH) if reach < line else (plane, 8, WIDTH)
        whole = added(pair_kernel, out, "pair_sum", whole, arrived)
    near = exchanged(whole, PLANE).reshape(128, WIDTH)
    far = lax.ppermute(near, CORE, swap)
    inverse, projection = factored(near, far, root)
    basis = dot(sample, inverse)
    return (basis, projection)


def solution(mesh):
    finer = Mesh(
        mesh.devices.reshape(4, 4, 2, mesh.shape["narrow"]),
        ("wide_0", "wide_1", "wide_2", "narrow"),
    )
    in_specs = (P(WIDE_NARROW, None), P())
    out_specs = (P(WIDE_NARROW, None), P())
    return jax.shard_map(on_device, mesh=finer, in_specs=in_specs, out_specs=out_specs, check_vma=False)
```

```python
import functools
import math

import jax
import jax.numpy as jnp
from jax import lax
from jax.experimental import pallas as pl
from jax.experimental.pallas import tpu as pltpu
from jax.sharding import Mesh
from jax.sharding import PartitionSpec as P

WIDE_NARROW = ("wide_0", "wide_1", "wide_2", "narrow")
PLANE = ("wide_0", "wide_1")
CORE = "wide_2"
LINE = "narrow"
HI = lax.Precision.HIGHEST
MID = lax.Precision.HIGH
F32 = jnp.float32
BF16 = jnp.bfloat16
BLOCK = 128
GRAM = 384
WIDTH = GRAM + 1024


def dot(a, b, dims=((1,), (0,)), precision=HI):
    return lax.dot_general(a, b, (dims, ((), ())), precision=precision, preferred_element_type=F32)


def dot16(a, b, dims=((1,), (0,))):
    return lax.dot_general(a, b, (dims, ((), ())), preferred_element_type=F32)


def two_sum(a, b):
    s = a + b
    t = s - a
    return s, (a - (s - t)) + (b - t)


def grid_slices(x, top):
    out = []
    for i in range(4):
        edge = top * (2.0 ** (17 - 8 * i))
        a = (x + edge) - edge
        out.append(a.astype(BF16))
        x = x - a
    return out


def half_gram(s, top, rows):
    tn = ((0,), (0,))
    h = l = low = None
    for at in range(0, s.shape[0], rows):
        a = grid_slices(s[at : at + rows, :], top)
        terms = [0.5 * dot16(a[0], a[0], tn), dot16(a[0], a[1], tn)]
        rest = (dot16(a[0], a[2], tn) + 0.5 * dot16(a[1], a[1], tn)) + (
            (dot16(a[0], a[3], tn) + dot16(a[1], a[2], tn)) + (dot16(a[1], a[3], tn) + 0.5 * dot16(a[2], a[2], tn))
        )
        low = rest if low is None else low + rest
        for t in terms:
            if h is None:
                h = t
            else:
                h, e = two_sum(h, t)
                low = low + e
    return two_sum(h, low)


def in_vmem(n):
    return [pl.BlockSpec(memory_space=pltpu.VMEM)] * n


def gram_kernel(sample_ref, terms_ref, mine_ref, other_ref, x_ref):
    top = jnp.max(jnp.abs(sample_ref[...]), axis=0, keepdims=True)
    h, l = half_gram(sample_ref, top, 1024)
    hi, e = two_sum(h, h.T)
    hi, lo = two_sum(hi, (l + l.T) + e)
    for i in range(2):
        at, mid = 128 * i, 128 + 64 * i
        x_ref[i, :, :128] = hi[at : at + 128, at : at + 128]
        x_ref[i, :, 128:256] = lo[at : at + 128, at : at + 128]
        x_ref[i, :, 256:320] = hi[:128, mid : mid + 64]
        x_ref[i, :, 320:] = lo[:128, mid : mid + 64]
    core = lax.axis_index(CORE)
    for half, ref in ((core, mine_ref), (1 - core, other_ref)):
        ref[:, :GRAM] = x_ref[half]
        ref[:, GRAM:] = terms_ref[pl.ds(pl.multiple_of(half * 128, 128), 128), :]


def local_halves(sample, terms):
    return pl.pallas_call(
        gram_kernel,
        in_specs=in_vmem(2),
        out_specs=in_vmem(2),
        out_shape=[jax.ShapeDtypeStruct((128, WIDTH), F32)] * 2,
        scratch_shapes=[pltpu.VMEM((2, 128, GRAM), F32)],
        compiler_params=pltpu.CompilerParams(vmem_limit_bytes=20 * 2**20),
        name="local_halves",
    )(sample, terms)


def total(parts):
    def compensated(x):
        error = 0.0
        while len(x) > 1:
            pairs = [two_sum(x[i], x[i + 1]) for i in range(0, len(x), 2)]
            error = error + functools.reduce(jnp.add, [e for _, e in pairs])
            x = [s for s, _ in pairs]
        return x[0], error

    def plain(x):
        while len(x) > 1:
            x = [x[i] + x[i + 1] for i in range(0, len(x), 2)]
        return x[0]

    hi, e = compensated([p[:, :128] for p in parts])
    lo = plain([p[:, 128:256] for p in parts]) + e
    mixed, e = compensated([p[:, 256:GRAM] for p in parts])
    lane = lax.broadcasted_iota(jnp.int32, mixed.shape, 1)
    mixed = jnp.where(lane < 64, mixed, mixed + pltpu.roll(e, 64, 1))
    return hi, lo, mixed, plain([p[:, GRAM:] for p in parts])


def store(ref, parts):
    at = 0
    for x in parts:
        ref[:, at : at + x.shape[1]] = x
        at += x.shape[1]


def pair_kernel(a_ref, b_ref, out_ref):
    s = total([a_ref[...], b_ref[...]])
    if len(out_ref.shape) == 2:
        store(out_ref, s)
    else:
        for i in range(out_ref.shape[0]):
            store(out_ref.at[i], s)


def stack_kernel(x_ref, out_ref):
    store(out_ref, total([x_ref[i] for i in range(x_ref.shape[0])]))


def added(kernel, shape, name, *parts):
    return pl.pallas_call(
        kernel,
        in_specs=in_vmem(len(parts)),
        out_specs=in_vmem(1)[0],
        out_shape=jax.ShapeDtypeStruct(shape, F32),
        compiler_params=pltpu.CompilerParams(vmem_limit_bytes=6 * 2**20),
        name=name,
    )(*parts)


def block_inverse(d):
    b = d.shape[0]
    shape = (8, 2 * b)
    row, col = (lax.broadcasted_iota(jnp.int32, (b, b), i) for i in (0, 1))
    m = jnp.concatenate([d, (row == col).astype(F32)], axis=1)
    nt = b // 8
    tiles = [m[8 * t : 8 * t + 8] for t in range(nt)]
    sub = lax.broadcasted_iota(jnp.int32, shape, 0)
    for t in range(nt):
        across = lambda x, j: jnp.broadcast_to(x[:, 8 * t + j : 8 * t + j + 1], shape)
        u = [jnp.broadcast_to(tiles[t][i : i + 1, :], shape) for i in range(8)]
        s = {(i, j): across(u[i], j) for i in range(8) for j in range(i, 8)}
        near = {v: [across(tiles[v], k) for k in range(8)] for v in range(t + 1, min(t + 2, nt))}
        l, scale = {}, []
        for k in range(8):
            rho = lax.rsqrt(s[k, k])
            scale.append(rho)
            for i in range(k + 1, 8):
                l[i, k] = s[k, i] * rho
            for i in range(k + 1, 8):
                for j in range(i, 8):
                    s[i, j] = s[i, j] - l[i, k] * l[j, k]
            for w in [u, *near.values()]:
                w[k] = w[k] * rho
                for i in range(k + 1, 8):
                    w[i] = w[i] - l[i, k] * w[k]
        out = u[0]
        for k in range(1, 8):
            out = jnp.where(sub == k, u[k], out)
        z = list(u)
        if t + 2 < nt:
            for k in range(7, -1, -1):
                z[k] = z[k] * scale[k]
                for i in range(k):
                    z[i] = z[i] - l[k, i] * z[k]
        for v in range(t + 1, nt):
            if v in near:
                p = [near[v][k] * u[k] for k in range(8)]
            else:
                p = [across(tiles[v], k) * z[k] for k in range(8)]
            while len(p) > 1:
                p = [p[i] + p[i + 1] for i in range(0, len(p), 2)]
            tiles[v] = tiles[v] - p[0]
        tiles[t] = out
    return jnp.concatenate(tiles, axis=0)[:, b:]


def factor_kernel(root, near_ref, far_ref, inverse_ref, projection_ref, x_ref, g_ref, w_ref, r_ref, y_ref, a_ref, m_ref, u_ref):
    n = 256
    core = lax.axis_index(CORE)
    for ref, half in ((near_ref, core), (far_ref, 1 - core)):
        x_ref[half] = ref[:, :GRAM]
        w_ref[pl.ds(pl.multiple_of(half * 128, 128), 128), :] = ref[:, GRAM:]
    for at in (0, 1):
        corner = [x_ref[i, :, 128 * at : 128 * at + 128] for i in (0, 1)]
        side = jnp.concatenate([x_ref[i, :, 256 + 64 * at : 320 + 64 * at] for i in (0, 1)], axis=1)
        g_ref[:128, n * at : n * at + 128] = corner[0]
        g_ref[:128, n * at + 128 : n * at + n] = side
        g_ref[128:, n * at : n * at + 128] = side.T
        g_ref[128:, n * at + 128 : n * at + n] = corner[1]
    row, col = (lax.broadcasted_iota(jnp.int32, (n, n), i) for i in (0, 1))
    eye = (row == col).astype(F32)
    lower = jnp.where(row > col, 1.0, jnp.where(row == col, 0.5, 0.0))

    a_ref[:, :n] = g_ref[:, :n]
    a_ref[:, n:] = eye
    r_ref[...] = jnp.zeros((n, n), F32)
    for lo in range(0, n, BLOCK):
        hi = lo + BLOCK
        p = dot(block_inverse(a_ref[lo:hi, lo:hi]), a_ref[lo:hi, :])
        r_ref[lo:hi, :] = p[:, :n]
        y_ref[lo:hi, :] = p[:, n:]
        if hi < n:
            a_ref[hi:, :] = a_ref[hi:, :] - dot(p[:, hi:n], p, ((0,), (0,)))
    r = jnp.where(row <= col, r_ref[...], 0.0)
    y = y_ref[...]

    tn, nt = ((0,), (0,)), ((1,), (1,))
    a = grid_slices(r, jnp.max(jnp.abs(r), axis=0, keepdims=True))
    both = lambda i, j: dot16(a[i], a[j], tn) + dot16(a[j], a[i], tn)
    d, e1 = two_sum(g_ref[:, :n], -dot16(a[0], a[0], tn))
    d, e2 = two_sum(d, -both(0, 1))
    fine = both(0, 2) + dot16(a[1], a[1], tn) + ((both(0, 3) + both(1, 2)) + (both(1, 3) + dot16(a[2], a[2], tn)))
    d = d + ((g_ref[:, n:] - fine) + (e1 + e2))

    f = dot(r, y, nt) - eye
    m = eye + ((f + f.T) + dot(f, f, tn, MID) + dot(dot(y, d, precision=MID), y, nt, MID))
    m_ref[...] = m
    u_ref[...] = eye - lower * (m - eye)

    def refine(carry):
        count, _ = carry
        u = u_ref[...]
        off = dot(dot(u, m_ref[...]), u, nt) - eye
        u_ref[...] = u - dot(lower * off, u, precision=MID)
        return count + 1, jnp.max(jnp.abs(off))

    lax.while_loop(lambda c: (c[0] < 24) & (c[1] > 1e-4), refine, (0, jnp.float32(1.0)))
    y = dot(u_ref[...], y)
    inverse_ref[...] = (y * root).T
    projection_ref[...] = dot(y * (1.0 / root), w_ref[...])


def factored(near, far, root):
    n = 256
    return pl.pallas_call(
        functools.partial(factor_kernel, root),
        in_specs=in_vmem(2),
        out_specs=in_vmem(2),
        out_shape=[jax.ShapeDtypeStruct((n, n), F32), jax.ShapeDtypeStruct((n, 1024), F32)],
        scratch_shapes=[
            pltpu.VMEM(s, F32) for s in ((2, 128, GRAM), (n, 512), (n, 1024), (n, n), (n, n), (n, 512), (n, n), (n, n))
        ],
        compiler_params=pltpu.CompilerParams(vmem_limit_bytes=16 * 2**20),
        name="factored",
    )(near, far)


def exchanged(x, axis):
    return lax.all_to_all(x, axis, 0, 0, tiled=True)


def on_device(corpus, sketch):
    plane, line = lax.axis_size(PLANE), lax.axis_size(LINE)
    total_rows = corpus.shape[0] * plane * line * lax.axis_size(CORE)
    root = math.sqrt(total_rows)
    swap = [(0, 1), (1, 0)]
    sample = dot(corpus, sketch)
    terms = dot(sample, corpus, ((0,), (0,)), MID)
    mine, other = local_halves(sample, terms)
    own = added(pair_kernel, mine.shape, "pair_sum", mine, lax.ppermute(other, CORE, swap))
    whole = added(stack_kernel, (8, WIDTH), "stack_sum", exchanged(own.reshape(plane, 8, WIDTH), PLANE))
    reach = 1
    while reach < line:
        flip = reach if 2 * reach < line else line - 1
        arrived = lax.ppermute(whole, LINE, [(i, i ^ flip) for i in range(line)])
        reach *= 2
        out = (8, WIDTH) if reach < line else (plane, 8, WIDTH)
        whole = added(pair_kernel, out, "pair_sum", whole, arrived)
    near = exchanged(whole, PLANE).reshape(128, WIDTH)
    far = lax.ppermute(near, CORE, swap)
    inverse, projection = factored(near, far, root)
    basis = dot(sample, inverse)
    return (basis, projection)


def solution(mesh):
    finer = Mesh(
        mesh.devices.reshape(4, 4, 2, mesh.shape["narrow"]),
        ("wide_0", "wide_1", "wide_2", "narrow"),
    )
    in_specs = (P(WIDE_NARROW, None), P())
    out_specs = (P(WIDE_NARROW, None), P())
    return jax.shard_map(on_device, mesh=finer, in_specs=in_specs, out_specs=out_specs, check_vma=False)
```

```python
import functools
import math

import jax
import jax.numpy as jnp
from jax import lax
from jax.experimental import pallas as pl
from jax.experimental.pallas import tpu as pltpu
from jax.sharding import Mesh
from jax.sharding import PartitionSpec as P

WIDE_NARROW = ("wide_0", "wide_1", "wide_2", "narrow")
PLANE = ("wide_0", "wide_1")
CORE = "wide_2"
LINE = "narrow"
HI = lax.Precision.HIGHEST
MID = lax.Precision.HIGH
F32 = jnp.float32
BF16 = jnp.bfloat16
BLOCK = 128
GRAM = 384
WIDTH = GRAM + 1024


def dot(a, b, dims=((1,), (0,)), precision=HI):
    return lax.dot_general(a, b, (dims, ((), ())), precision=precision, preferred_element_type=F32)


def dot16(a, b, dims=((1,), (0,))):
    return lax.dot_general(a, b, (dims, ((), ())), preferred_element_type=F32)


def two_sum(a, b):
    s = a + b
    t = s - a
    return s, (a - (s - t)) + (b - t)


def grid_slices(x, top):
    out = []
    for i in range(4):
        edge = top * (2.0 ** (17 - 8 * i))
        a = (x + edge) - edge
        out.append(a.astype(BF16))
        x = x - a
    return out


def half_gram(s, top, rows):
    tn = ((0,), (0,))
    h = l = low = None
    for at in range(0, s.shape[0], rows):
        a = grid_slices(s[at : at + rows, :], top)
        terms = [0.5 * dot16(a[0], a[0], tn), dot16(a[0], a[1], tn)]
        rest = (dot16(a[0], a[2], tn) + 0.5 * dot16(a[1], a[1], tn)) + (
            (dot16(a[0], a[3], tn) + dot16(a[1], a[2], tn)) + (dot16(a[1], a[3], tn) + 0.5 * dot16(a[2], a[2], tn))
        )
        low = rest if low is None else low + rest
        for t in terms:
            if h is None:
                h = t
            else:
                h, e = two_sum(h, t)
                low = low + e
    return two_sum(h, low)


def in_vmem(n):
    return [pl.BlockSpec(memory_space=pltpu.VMEM)] * n


def gram_kernel(sample_ref, mine_ref, other_ref, x_ref):
    top = jnp.max(jnp.abs(sample_ref[...]), axis=0, keepdims=True)
    h, l = half_gram(sample_ref, top, 1024)
    hi, e = two_sum(h, h.T)
    hi, lo = two_sum(hi, (l + l.T) + e)
    for i in range(2):
        at, mid = 128 * i, 128 + 64 * i
        x_ref[i, :, :128] = hi[at : at + 128, at : at + 128]
        x_ref[i, :, 128:256] = lo[at : at + 128, at : at + 128]
        x_ref[i, :, 256:320] = hi[:128, mid : mid + 64]
        x_ref[i, :, 320:] = lo[:128, mid : mid + 64]
    core = lax.axis_index(CORE)
    mine_ref[...] = x_ref[core]
    other_ref[...] = x_ref[1 - core]


def halves_kernel(terms_ref, mine_ref, other_ref):
    core = lax.axis_index(CORE)
    for half, ref in ((core, mine_ref), (1 - core, other_ref)):
        ref[...] = terms_ref[pl.ds(pl.multiple_of(half * 128, 128), 128), :]


def local_halves(kernel, x, width, name, scratch, mib):
    return pl.pallas_call(
        kernel,
        in_specs=in_vmem(1),
        out_specs=in_vmem(2),
        out_shape=[jax.ShapeDtypeStruct((128, width), F32)] * 2,
        scratch_shapes=scratch,
        compiler_params=pltpu.CompilerParams(vmem_limit_bytes=mib * 2**20),
        name=name,
    )(x)


def total(parts):
    def compensated(x):
        error = 0.0
        while len(x) > 1:
            pairs = [two_sum(x[i], x[i + 1]) for i in range(0, len(x), 2)]
            error = error + functools.reduce(jnp.add, [e for _, e in pairs])
            x = [s for s, _ in pairs]
        return x[0], error

    def plain(x):
        while len(x) > 1:
            x = [x[i] + x[i + 1] for i in range(0, len(x), 2)]
        return x[0]

    hi, e = compensated([p[:, :128] for p in parts])
    lo = plain([p[:, 128:256] for p in parts]) + e
    mixed, e = compensated([p[:, 256:GRAM] for p in parts])
    lane = lax.broadcasted_iota(jnp.int32, mixed.shape, 1)
    mixed = jnp.where(lane < 64, mixed, mixed + pltpu.roll(e, 64, 1))
    return hi, lo, mixed, plain([p[:, GRAM:] for p in parts])


def store(ref, parts):
    at = 0
    for x in parts:
        ref[:, at : at + x.shape[1]] = x
        at += x.shape[1]


def core_kernel(gram_ref, far_gram_ref, terms_ref, far_terms_ref, out_ref):
    far = jnp.concatenate([far_gram_ref[...], far_terms_ref[...]], axis=1)
    store(out_ref, total([jnp.concatenate([gram_ref[...], terms_ref[...]], axis=1), far]))


def pair_kernel(a_ref, b_ref, out_ref):
    s = total([a_ref[...], b_ref[...]])
    if len(out_ref.shape) == 2:
        store(out_ref, s)
    else:
        for i in range(out_ref.shape[0]):
            store(out_ref.at[i], s)


def stack_kernel(x_ref, out_ref):
    store(out_ref, total([x_ref[i] for i in range(x_ref.shape[0])]))


def added(kernel, shape, name, *parts):
    return pl.pallas_call(
        kernel,
        in_specs=in_vmem(len(parts)),
        out_specs=in_vmem(1)[0],
        out_shape=jax.ShapeDtypeStruct(shape, F32),
        compiler_params=pltpu.CompilerParams(vmem_limit_bytes=6 * 2**20),
        name=name,
    )(*parts)


def block_inverse(d):
    b = d.shape[0]
    shape = (8, 2 * b)
    row, col = (lax.broadcasted_iota(jnp.int32, (b, b), i) for i in (0, 1))
    m = jnp.concatenate([d, (row == col).astype(F32)], axis=1)
    nt = b // 8
    tiles = [m[8 * t : 8 * t + 8] for t in range(nt)]
    sub = lax.broadcasted_iota(jnp.int32, shape, 0)
    for t in range(nt):
        across = lambda x, j: jnp.broadcast_to(x[:, 8 * t + j : 8 * t + j + 1], shape)
        u = [jnp.broadcast_to(tiles[t][i : i + 1, :], shape) for i in range(8)]
        s = {(i, j): across(u[i], j) for i in range(8) for j in range(i, 8)}
        near = {v: [across(tiles[v], k) for k in range(8)] for v in range(t + 1, min(t + 2, nt))}
        l, scale = {}, []
        for k in range(8):
            rho = lax.rsqrt(s[k, k])
            scale.append(rho)
            for i in range(k + 1, 8):
                l[i, k] = s[k, i] * rho
            for i in range(k + 1, 8):
                for j in range(i, 8):
                    s[i, j] = s[i, j] - l[i, k] * l[j, k]
            for w in [u, *near.values()]:
                w[k] = w[k] * rho
                for i in range(k + 1, 8):
                    w[i] = w[i] - l[i, k] * w[k]
        out = u[0]
        for k in range(1, 8):
            out = jnp.where(sub == k, u[k], out)
        z = list(u)
        if t + 2 < nt:
            for k in range(7, -1, -1):
                z[k] = z[k] * scale[k]
                for i in range(k):
                    z[i] = z[i] - l[k, i] * z[k]
        for v in range(t + 1, nt):
            if v in near:
                p = [near[v][k] * u[k] for k in range(8)]
            else:
                p = [across(tiles[v], k) * z[k] for k in range(8)]
            while len(p) > 1:
                p = [p[i] + p[i + 1] for i in range(0, len(p), 2)]
            tiles[v] = tiles[v] - p[0]
        tiles[t] = out
    return jnp.concatenate(tiles, axis=0)[:, b:]


def factor_kernel(root, near_ref, far_ref, inverse_ref, projection_ref, x_ref, g_ref, w_ref, r_ref, y_ref, a_ref, m_ref, u_ref):
    n = 256
    core = lax.axis_index(CORE)
    for ref, half in ((near_ref, core), (far_ref, 1 - core)):
        x_ref[half] = ref[:, :GRAM]
        w_ref[pl.ds(pl.multiple_of(half * 128, 128), 128), :] = ref[:, GRAM:]
    for at in (0, 1):
        corner = [x_ref[i, :, 128 * at : 128 * at + 128] for i in (0, 1)]
        side = jnp.concatenate([x_ref[i, :, 256 + 64 * at : 320 + 64 * at] for i in (0, 1)], axis=1)
        g_ref[:128, n * at : n * at + 128] = corner[0]
        g_ref[:128, n * at + 128 : n * at + n] = side
        g_ref[128:, n * at : n * at + 128] = side.T
        g_ref[128:, n * at + 128 : n * at + n] = corner[1]
    row, col = (lax.broadcasted_iota(jnp.int32, (n, n), i) for i in (0, 1))
    eye = (row == col).astype(F32)
    lower = jnp.where(row > col, 1.0, jnp.where(row == col, 0.5, 0.0))

    a_ref[:, :n] = g_ref[:, :n]
    a_ref[:, n:] = eye
    r_ref[...] = jnp.zeros((n, n), F32)
    y_ref[...] = jnp.zeros((n, n), F32)
    for lo in range(0, n, BLOCK):
        hi = lo + BLOCK
        p = dot(block_inverse(a_ref[lo:hi, lo:hi]), a_ref[lo:hi, lo : n + hi])
        r_ref[lo:hi, lo:] = p[:, : n - lo]
        y_ref[lo:hi, :hi] = p[:, n - lo :]
        if hi < n:
            a_ref[hi:, hi : n + hi] = a_ref[hi:, hi : n + hi] - dot(p[:, BLOCK : n - lo], p[:, BLOCK:], ((0,), (0,)))
    r = jnp.where(row <= col, r_ref[...], 0.0)
    y = y_ref[...]

    tn, nt = ((0,), (0,)), ((1,), (1,))
    a = grid_slices(r, jnp.max(jnp.abs(r), axis=0, keepdims=True))
    both = lambda i, j: dot16(a[i], a[j], tn) + dot16(a[j], a[i], tn)
    d, e1 = two_sum(g_ref[:, :n], -dot16(a[0], a[0], tn))
    d, e2 = two_sum(d, -both(0, 1))
    fine = both(0, 2) + dot16(a[1], a[1], tn) + ((both(0, 3) + both(1, 2)) + (both(1, 3) + dot16(a[2], a[2], tn)))
    d = d + ((g_ref[:, n:] - fine) + (e1 + e2))

    f = dot(r, y, nt) - eye
    m = eye + ((f + f.T) + dot(f, f, tn, MID) + dot(dot(y, d, precision=MID), y, nt, MID))
    m_ref[...] = m
    u_ref[...] = eye - lower * (m - eye)

    def refine(carry):
        count, _ = carry
        u = u_ref[...]
        off = dot(dot(u, m_ref[...]), u, nt) - eye
        u_ref[...] = u - dot(lower * off, u, precision=MID)
        return count + 1, jnp.max(jnp.abs(off))

    lax.while_loop(lambda c: (c[0] < 24) & (c[1] > 1e-4), refine, (0, jnp.float32(1.0)))
    y = dot(u_ref[...], y)
    inverse_ref[...] = (y * root).T
    projection_ref[...] = dot(y * (1.0 / root), w_ref[...])


def factored(near, far, root):
    n = 256
    return pl.pallas_call(
        functools.partial(factor_kernel, root),
        in_specs=in_vmem(2),
        out_specs=in_vmem(2),
        out_shape=[jax.ShapeDtypeStruct((n, n), F32), jax.ShapeDtypeStruct((n, 1024), F32)],
        scratch_shapes=[
            pltpu.VMEM(s, F32) for s in ((2, 128, GRAM), (n, 512), (n, 1024), (n, n), (n, n), (n, 512), (n, n), (n, n))
        ],
        compiler_params=pltpu.CompilerParams(vmem_limit_bytes=16 * 2**20),
        name="factored",
    )(near, far)


def exchanged(x, axis):
    return lax.all_to_all(x, axis, 0, 0, tiled=True)


def on_device(corpus, sketch):
    plane, line = lax.axis_size(PLANE), lax.axis_size(LINE)
    total_rows = corpus.shape[0] * plane * line * lax.axis_size(CORE)
    root = math.sqrt(total_rows)
    swap = [(0, 1), (1, 0)]
    sample = dot(corpus, sketch)
    terms = dot(sample, corpus, ((0,), (0,)), MID)
    terms, other_terms = local_halves(halves_kernel, terms, 1024, "term_halves", [], 4)
    far_terms = lax.ppermute(other_terms, CORE, swap)
    gram, other_gram = local_halves(gram_kernel, sample, GRAM, "gram_halves", [pltpu.VMEM((2, 128, GRAM), F32)], 20)
    far_gram = lax.ppermute(other_gram, CORE, swap)
    own = added(core_kernel, (128, WIDTH), "core_sum", gram, far_gram, terms, far_terms)
    whole = added(stack_kernel, (8, WIDTH), "stack_sum", exchanged(own.reshape(plane, 8, WIDTH), PLANE))
    reach = 1
    while reach < line:
        flip = reach if 2 * reach < line else line - 1
        arrived = lax.ppermute(whole, LINE, [(i, i ^ flip) for i in range(line)])
        reach *= 2
        out = (8, WIDTH) if reach < line else (plane, 8, WIDTH)
        whole = added(pair_kernel, out, "pair_sum", whole, arrived)
    near = exchanged(whole, PLANE).reshape(128, WIDTH)
    far = lax.ppermute(near, CORE, swap)
    inverse, projection = factored(near, far, root)
    basis = dot(sample, inverse)
    return (basis, projection)


def solution(mesh):
    finer = Mesh(
        mesh.devices.reshape(4, 4, 2, mesh.shape["narrow"]),
        ("wide_0", "wide_1", "wide_2", "narrow"),
    )
    in_specs = (P(WIDE_NARROW, None), P())
    out_specs = (P(WIDE_NARROW, None), P())
    return jax.shard_map(on_device, mesh=finer, in_specs=in_specs, out_specs=out_specs, check_vma=False)
```

```python
import functools
import math

import jax
import jax.numpy as jnp
from jax import lax
from jax.experimental import pallas as pl
from jax.experimental.pallas import tpu as pltpu
from jax.sharding import Mesh
from jax.sharding import PartitionSpec as P

WIDE_NARROW = ("wide_0", "wide_1", "wide_2", "narrow")
PLANE = ("wide_0", "wide_1")
CORE = "wide_2"
LINE = "narrow"
HI = lax.Precision.HIGHEST
MID = lax.Precision.HIGH
F32 = jnp.float32
BF16 = jnp.bfloat16
BLOCK = 128
GRAM = 384
WIDTH = GRAM + 1024


def dot(a, b, dims=((1,), (0,)), precision=HI):
    return lax.dot_general(a, b, (dims, ((), ())), precision=precision, preferred_element_type=F32)


def dot16(a, b, dims=((1,), (0,))):
    return lax.dot_general(a, b, (dims, ((), ())), preferred_element_type=F32)


def two_sum(a, b):
    s = a + b
    t = s - a
    return s, (a - (s - t)) + (b - t)


def grid_slices(x, top):
    out = []
    for i in range(4):
        edge = top * (2.0 ** (17 - 8 * i))
        a = (x + edge) - edge
        out.append(a.astype(BF16))
        x = x - a
    return out


def half_gram(s, top, rows):
    tn = ((0,), (0,))
    h = l = low = None
    for at in range(0, s.shape[0], rows):
        a = grid_slices(s[at : at + rows, :], top)
        terms = [0.5 * dot16(a[0], a[0], tn), dot16(a[0], a[1], tn)]
        rest = (dot16(a[0], a[2], tn) + 0.5 * dot16(a[1], a[1], tn)) + (
            (dot16(a[0], a[3], tn) + dot16(a[1], a[2], tn)) + (dot16(a[1], a[3], tn) + 0.5 * dot16(a[2], a[2], tn))
        )
        low = rest if low is None else low + rest
        for t in terms:
            if h is None:
                h = t
            else:
                h, e = two_sum(h, t)
                low = low + e
    return two_sum(h, low)


def in_vmem(n):
    return [pl.BlockSpec(memory_space=pltpu.VMEM)] * n


def gram_kernel(sample_ref, mine_ref, other_ref, x_ref):
    top = jnp.max(jnp.abs(sample_ref[...]), axis=0, keepdims=True)
    h, l = half_gram(sample_ref, top, 1024)
    hi, e = two_sum(h, h.T)
    hi, lo = two_sum(hi, (l + l.T) + e)
    for i in range(2):
        at, mid = 128 * i, 128 + 64 * i
        x_ref[i, :, :128] = hi[at : at + 128, at : at + 128]
        x_ref[i, :, 128:256] = lo[at : at + 128, at : at + 128]
        x_ref[i, :, 256:320] = hi[:128, mid : mid + 64]
        x_ref[i, :, 320:] = lo[:128, mid : mid + 64]
    core = lax.axis_index(CORE)
    mine_ref[...] = x_ref[core]
    other_ref[...] = x_ref[1 - core]


def halves_kernel(terms_ref, mine_ref, other_ref):
    core = lax.axis_index(CORE)
    for half, ref in ((core, mine_ref), (1 - core, other_ref)):
        ref[...] = terms_ref[pl.ds(pl.multiple_of(half * 128, 128), 128), :]


def local_halves(kernel, x, width, name, scratch, mib):
    return pl.pallas_call(
        kernel,
        in_specs=in_vmem(1),
        out_specs=in_vmem(2),
        out_shape=[jax.ShapeDtypeStruct((128, width), F32)] * 2,
        scratch_shapes=scratch,
        compiler_params=pltpu.CompilerParams(vmem_limit_bytes=mib * 2**20),
        name=name,
    )(x)


def total(parts):
    def compensated(x):
        error = 0.0
        while len(x) > 1:
            pairs = [two_sum(x[i], x[i + 1]) for i in range(0, len(x), 2)]
            error = error + functools.reduce(jnp.add, [e for _, e in pairs])
            x = [s for s, _ in pairs]
        return x[0], error

    def plain(x):
        while len(x) > 1:
            x = [x[i] + x[i + 1] for i in range(0, len(x), 2)]
        return x[0]

    hi, e = compensated([p[:, :128] for p in parts])
    lo = plain([p[:, 128:256] for p in parts]) + e
    mixed, e = compensated([p[:, 256:GRAM] for p in parts])
    lane = lax.broadcasted_iota(jnp.int32, mixed.shape, 1)
    mixed = jnp.where(lane < 64, mixed, mixed + pltpu.roll(e, 64, 1))
    return hi, lo, mixed, plain([p[:, GRAM:] for p in parts])


def store(ref, parts):
    at = 0
    for x in parts:
        ref[:, at : at + x.shape[1]] = x
        at += x.shape[1]


def core_kernel(gram_ref, far_gram_ref, terms_ref, far_terms_ref, out_ref):
    far = jnp.concatenate([far_gram_ref[...], far_terms_ref[...]], axis=1)
    store(out_ref, total([jnp.concatenate([gram_ref[...], terms_ref[...]], axis=1), far]))


def pair_kernel(a_ref, b_ref, out_ref):
    s = total([a_ref[...], b_ref[...]])
    if len(out_ref.shape) == 2:
        store(out_ref, s)
    else:
        for i in range(out_ref.shape[0]):
            store(out_ref.at[i], s)


def stack_kernel(x_ref, out_ref):
    store(out_ref, total([x_ref[i] for i in range(x_ref.shape[0])]))


def added(kernel, shape, name, *parts):
    return pl.pallas_call(
        kernel,
        in_specs=in_vmem(len(parts)),
        out_specs=in_vmem(1)[0],
        out_shape=jax.ShapeDtypeStruct(shape, F32),
        compiler_params=pltpu.CompilerParams(vmem_limit_bytes=6 * 2**20),
        name=name,
    )(*parts)


def block_inverse(d):
    b = d.shape[0]
    shape = (8, 2 * b)
    row, col = (lax.broadcasted_iota(jnp.int32, (b, b), i) for i in (0, 1))
    m = jnp.concatenate([d, (row == col).astype(F32)], axis=1)
    nt = b // 8
    tiles = [m[8 * t : 8 * t + 8] for t in range(nt)]
    sub = lax.broadcasted_iota(jnp.int32, shape, 0)
    for t in range(nt):
        across = lambda x, j: jnp.broadcast_to(x[:, 8 * t + j : 8 * t + j + 1], shape)
        u = [jnp.broadcast_to(tiles[t][i : i + 1, :], shape) for i in range(8)]
        s = {(i, j): across(u[i], j) for i in range(8) for j in range(i, 8)}
        near = {v: [across(tiles[v], k) for k in range(8)] for v in range(t + 1, min(t + 2, nt))}
        l, scale = {}, []
        for k in range(8):
            rho = lax.rsqrt(s[k, k])
            scale.append(rho)
            for i in range(k + 1, 8):
                l[i, k] = s[k, i] * rho
            for i in range(k + 1, 8):
                for j in range(i, 8):
                    s[i, j] = s[i, j] - l[i, k] * l[j, k]
            for w in [u, *near.values()]:
                w[k] = w[k] * rho
                for i in range(k + 1, 8):
                    w[i] = w[i] - l[i, k] * w[k]
        out = u[0]
        for k in range(1, 8):
            out = jnp.where(sub == k, u[k], out)
        z = list(u)
        if t + 2 < nt:
            for k in range(7, -1, -1):
                z[k] = z[k] * scale[k]
                for i in range(k):
                    z[i] = z[i] - l[k, i] * z[k]
        for v in range(t + 1, nt):
            if v in near:
                p = [near[v][k] * u[k] for k in range(8)]
            else:
                p = [across(tiles[v], k) * z[k] for k in range(8)]
            while len(p) > 1:
                p = [p[i] + p[i + 1] for i in range(0, len(p), 2)]
            tiles[v] = tiles[v] - p[0]
        tiles[t] = out
    return jnp.concatenate(tiles, axis=0)[:, b:]


def factor_kernel(root, near_ref, far_ref, inverse_ref, projection_ref, x_ref, g_ref, w_ref, r_ref, y_ref, a_ref, m_ref, u_ref):
    n = 256
    core = lax.axis_index(CORE)
    for ref, half in ((near_ref, core), (far_ref, 1 - core)):
        x_ref[half] = ref[:, :GRAM]
        w_ref[pl.ds(pl.multiple_of(half * 128, 128), 128), :] = ref[:, GRAM:]
    for at in (0, 1):
        corner = [x_ref[i, :, 128 * at : 128 * at + 128] for i in (0, 1)]
        side = jnp.concatenate([x_ref[i, :, 256 + 64 * at : 320 + 64 * at] for i in (0, 1)], axis=1)
        g_ref[:128, n * at : n * at + 128] = corner[0]
        g_ref[:128, n * at + 128 : n * at + n] = side
        g_ref[128:, n * at : n * at + 128] = side.T
        g_ref[128:, n * at + 128 : n * at + n] = corner[1]
    row, col = (lax.broadcasted_iota(jnp.int32, (n, n), i) for i in (0, 1))
    eye = (row == col).astype(F32)
    lower = jnp.where(row > col, 1.0, jnp.where(row == col, 0.5, 0.0))

    a_ref[:, :n] = g_ref[:, :n]
    a_ref[:, n:] = eye
    r_ref[...] = jnp.zeros((n, n), F32)
    for lo in range(0, n, BLOCK):
        hi = lo + BLOCK
        p = dot(block_inverse(a_ref[lo:hi, lo:hi]), a_ref[lo:hi, :])
        r_ref[lo:hi, :] = p[:, :n]
        y_ref[lo:hi, :] = p[:, n:]
        if hi < n:
            a_ref[hi:, :] = a_ref[hi:, :] - dot(p[:, hi:n], p, ((0,), (0,)))
    r = jnp.where(row <= col, r_ref[...], 0.0)
    y = y_ref[...]

    tn, nt = ((0,), (0,)), ((1,), (1,))
    a = grid_slices(r, jnp.max(jnp.abs(r), axis=0, keepdims=True))
    both = lambda i, j: dot16(a[i], a[j], tn) + dot16(a[j], a[i], tn)
    d, e1 = two_sum(g_ref[:, :n], -dot16(a[0], a[0], tn))
    d, e2 = two_sum(d, -both(0, 1))
    fine = both(0, 2) + dot16(a[1], a[1], tn) + ((both(0, 3) + both(1, 2)) + (both(1, 3) + dot16(a[2], a[2], tn)))
    d = d + ((g_ref[:, n:] - fine) + (e1 + e2))

    f = dot(r, y, nt) - eye
    m = (f + f.T) + dot(f, f, tn, MID) + dot(dot(y, d, precision=MID), y, nt, MID)
    m_ref[...] = m
    u_ref[...] = lower * m

    def refine(carry):
        count, _ = carry
        u, m = u_ref[...], m_ref[...]
        um = dot(u, m, precision=MID)
        once = u + um
        off = ((m - once) - once.T) + (dot(u, u, nt, MID) + dot(um, u, nt, MID))
        step = lower * off
        u_ref[...] = u + (step - dot(step, u, precision=MID))
        return count + 1, jnp.max(jnp.abs(off))

    lax.while_loop(lambda c: (c[0] < 24) & (c[1] > 1e-4), refine, (0, jnp.float32(1.0)))
    y = y - dot(u_ref[...], y)
    inverse_ref[...] = (y * root).T
    projection_ref[...] = dot(y * (1.0 / root), w_ref[...])


def factored(near, far, root):
    n = 256
    return pl.pallas_call(
        functools.partial(factor_kernel, root),
        in_specs=in_vmem(2),
        out_specs=in_vmem(2),
        out_shape=[jax.ShapeDtypeStruct((n, n), F32), jax.ShapeDtypeStruct((n, 1024), F32)],
        scratch_shapes=[
            pltpu.VMEM(s, F32) for s in ((2, 128, GRAM), (n, 512), (n, 1024), (n, n), (n, n), (n, 512), (n, n), (n, n))
        ],
        compiler_params=pltpu.CompilerParams(vmem_limit_bytes=16 * 2**20),
        name="factored",
    )(near, far)


def exchanged(x, axis):
    return lax.all_to_all(x, axis, 0, 0, tiled=True)


def on_device(corpus, sketch):
    plane, line = lax.axis_size(PLANE), lax.axis_size(LINE)
    total_rows = corpus.shape[0] * plane * line * lax.axis_size(CORE)
    root = math.sqrt(total_rows)
    swap = [(0, 1), (1, 0)]
    sample = dot(corpus, sketch)
    terms = dot(sample, corpus, ((0,), (0,)), MID)
    terms, other_terms = local_halves(halves_kernel, terms, 1024, "term_halves", [], 4)
    far_terms = lax.ppermute(other_terms, CORE, swap)
    gram, other_gram = local_halves(gram_kernel, sample, GRAM, "gram_halves", [pltpu.VMEM((2, 128, GRAM), F32)], 20)
    far_gram = lax.ppermute(other_gram, CORE, swap)
    own = added(core_kernel, (128, WIDTH), "core_sum", gram, far_gram, terms, far_terms)
    whole = added(stack_kernel, (8, WIDTH), "stack_sum", exchanged(own.reshape(plane, 8, WIDTH), PLANE))
    reach = 1
    while reach < line:
        flip = reach if 2 * reach < line else line - 1
        arrived = lax.ppermute(whole, LINE, [(i, i ^ flip) for i in range(line)])
        reach *= 2
        out = (8, WIDTH) if reach < line else (plane, 8, WIDTH)
        whole = added(pair_kernel, out, "pair_sum", whole, arrived)
    near = exchanged(whole, PLANE).reshape(128, WIDTH)
    far = lax.ppermute(near, CORE, swap)
    inverse, projection = factored(near, far, root)
    basis = dot(sample, inverse)
    return (basis, projection)


def solution(mesh):
    finer = Mesh(
        mesh.devices.reshape(4, 4, 2, mesh.shape["narrow"]),
        ("wide_0", "wide_1", "wide_2", "narrow"),
    )
    in_specs = (P(WIDE_NARROW, None), P())
    out_specs = (P(WIDE_NARROW, None), P())
    return jax.shard_map(on_device, mesh=finer, in_specs=in_specs, out_specs=out_specs, check_vma=False)
```
